32 devices in a mesh: req: 8 (over z, y), kv: 4 (over x, core).
Axes of the slice: x: 2, y: 2, z: 4, core: 2. Of those that a mesh axis runs over, the one named last changes fastest.
Arguments:
- tokens: bfloat16 [8, 128, 2880], P('req'), may hold values from -6 to 6
- attn_gain: float32 [2880], replicated, may hold values from 0.1 to 1.9
- w_qkv: bfloat16 [2880, 5120], P(None, 'kv'), may hold values from -0.109375 to 0.109375
- sink_logits: float32 [64], P('kv'), may hold values from 0 to 10
- w_out: bfloat16 [4096, 2880], P('kv'), may hold values from -0.09375 to 0.09375
- kv_cache: bfloat16 [1024, 128, 1024], P('req', None, 'kv'), may hold values from -102 to 102
- page_table: int32 [8, 128], P('req'), may hold values from 0 to 127, each once within a row
- cache_lengths: int32 [8], P('req'), may hold values from 0 to 16384, as said below
- moe_gain: float32 [2880], replicated, may hold values from 0.1 to 1.9
- routes: int32 [8, 128, 4], P('req'), may hold values from 0 to 15, all different within a row; in each aligned block of 32 rows (0 to 31, 32 to 63, ..., all dimensions but the last counted through in order) at most 12 rows name the same one
- gate_weights: float32 [8, 128, 4], P('req'), may hold values from 0.1 to 0.7
- w_gate_up: bfloat16 [16, 2, 2880, 2880], P('req', None, None, 'kv'), may hold values from -0.109375 to 0.109375
- w_down: bfloat16 [16, 2880, 2880], P('req', 'kv'), may hold values from -0.109375 to 0.109375
Outputs:
- layer_out: bfloat16 [8, 128, 2880], P('req', 'kv')
The draws below stay inside these ranges and needn't reach their ends.
Inputs may be any that keep to these rules, and one draw needn't show every extreme that they name: `routes`: each token names 4 different experts. In each aligned block of 32 tokens (requests first, then new tokens) no expert is named by more than 12 tokens, and some block reaches 12. `page_table`: each row names every one of its request's 128 pages once. `cache_lengths`: some request's cache is full.
All inputs are finite; a program needn't handle non-finite values.
Results may differ from the reference program's by a relative error of at most 0.014.
Values may be sent and summed in bfloat16 or wider, within the bound.
A program may use at most 192 MiB of HBM per device.

```python
import math
import jax
import jax.numpy as jnp
import numpy as np
from jax import lax

D = 2880
QH = 64
KVH = 8
HD = 64
FF = 2880
TOP = 4
PAGE = 128
NEW_TOK = 128
PAGES_DEV = 128
GROUP = 8
EXPERTS = 16
REQS = 8
POOL = 1024
CTX = 16384
ROWS_DEV = 32
CAP = 12
N_REQ = 8
N_KV = 4


def draw_kv_cache(key, part):
    base_key = jax.random.fold_in(key, 11)
    entries = jnp.clip(jax.random.normal(base_key, (POOL, PAGE, KVH, 2, HD), jnp.float32), -4.0, 4.0)
    return entries.reshape(POOL, PAGE, KVH * 2 * HD).astype(jnp.bfloat16)


def draw_cache_lengths(key, part):
    value_key = jax.random.fold_in(key, 21)
    place_key = jax.random.fold_in(key, 22)
    drawn = jax.random.randint(value_key, (REQS,), 0, CTX + 1)
    longest = jax.random.randint(place_key, (), 0, REQS)
    return jnp.where(jnp.arange(REQS) == longest, CTX, drawn).astype(jnp.int32)


def levels(own_key, shape, shards, least, top_value):
    factor_of, own = 1.0, jax.random.fold_in(own_key, 6)
    for axis_at, blocks in shards:
        draws = jnp.exp(jax.random.uniform(jax.random.fold_in(own, axis_at), (blocks,), jnp.float32, least / len(shards), top_value / len(shards)))
        factor_of = factor_of * jnp.repeat(draws, shape[axis_at] // blocks).reshape([-1 if axis == axis_at else 1 for axis in range(len(shape))])
    return factor_of


def routed_block(rng, own, number, rows, count, top, most, slope):
    sequence = jax.random.permutation(rng, count)
    crowded, usual = portions_of(count, rows * top, most, slope, True), portions_of(count, rows * top, most, slope, False)
    places = jnp.arange(count)

    def named(tallies, turn):
        used = int((tallies > 0).sum())
        fixed = max(1, used // 4)
        passed = fixed + (places - fixed + turn * (used - fixed)) % max(1, count - fixed)
        return jnp.zeros((count,), jnp.int32).at[sequence[jnp.where(places < fixed, places, passed)]].set(jnp.asarray(tallies, jnp.int32))

    tallies = jnp.where(number % 4 == 0, named(crowded, number // 4), named(usual, number - number // 4 - 1))
    mixed = jax.random.permutation(jax.random.fold_in(own, 3), count)
    donor, taker = mixed[0:count // 2 * 2:2], mixed[1:count // 2 * 2:2]
    slack = jnp.minimum(tallies[donor] - 1, most - tallies[taker]) // 2
    slack = jnp.where((donor == sequence[0]) | (taker == sequence[0]) | (tallies[taker] == 0), 0, jnp.maximum(slack, 0))
    passed = jax.random.randint(jax.random.fold_in(own, 4), (count // 2,), 0, 1 << 20) % (slack + 1)
    tallies = tallies.at[donor].add(-passed).at[taker].add(passed)
    members = jnp.searchsorted(jnp.cumsum(tallies), jnp.arange(rows * top), side="right").astype(jnp.int32)
    listing = members.reshape(top, rows).T
    listing = listing[jax.random.permutation(jax.random.fold_in(own, 1), rows)]
    turn = jax.random.randint(jax.random.fold_in(own, 2), (rows, 1), 0, top)
    return jnp.take_along_axis(listing, (jnp.arange(top)[None, :] + turn) % top, axis=1)


def portions_of(number_of, total, limit, slope, full):
    portions = [(1 << 20) // math.isqrt(standing ** slope) + 1 for standing in range(1, number_of + 1)]
    largest = limit if full else min(limit, max(-(-total // number_of), total * portions[0] // sum(portions)))
    least = 1 if total - largest >= number_of - 1 else 0
    counts, surplus = [largest] + [least] * (number_of - 1), total - largest - least * (number_of - 1)
    while surplus > 0:
        candidates = [i for i in range(1, number_of) if counts[i] < largest] or [i for i in range(1, number_of) if counts[i] < limit]
        mass, remaining = sum([portions[i] for i in candidates]), surplus
        for i in candidates:
            addition = min(limit - counts[i], max(1, remaining * portions[i] // mass), surplus)
            counts[i] = counts[i] + addition
            surplus = surplus - addition
    return np.array(counts)


def gaussian(own_key, shape, spread, reach, split=(), kind=jnp.bfloat16):
    values = jax.random.normal(own_key, shape, jnp.float32) * spread
    if len(split) > 0:
        values = levels(own_key, shape, split, -0.22, 0.18) * values
    return jnp.clip(values, min=-reach, max=reach).astype(kind)


def setup_inputs(seed: int = 0) -> dict:
    splits = jax.random.split(jax.random.key(seed), 14)
    tokens = gaussian(splits[0], (REQS, NEW_TOK, D), 1.0, 6.0, ((0, 8),))
    attn_gain = jnp.clip(1.0 + 0.18 * jax.random.normal(splits[1], (D,), jnp.float32), 0.1, 1.9)
    w_qkv = gaussian(splits[2], (D, KVH * (GROUP + 2) * HD), D ** -0.5, 0.109375, ((1, 4),))
    sink_logits = jnp.clip(10.0 * jax.random.uniform(splits[3], (QH,), jnp.float32) ** levels(splits[3], (QH,), ((0, 4),), -0.2, 0.2), 0.0, 10.0)
    w_out = gaussian(splits[4], (QH * HD, D), (QH * HD) ** -0.5, 0.09375, ((0, 4),))
    kv_cache = draw_kv_cache(jax.random.fold_in(splits[13], 71), 0)
    page_table = jax.vmap(lambda own: jax.random.permutation(own, PAGES_DEV))(jax.random.split(splits[6], REQS)).reshape((REQS, PAGES_DEV)).astype(jnp.int32)
    cache_lengths = draw_cache_lengths(jax.random.fold_in(splits[13], 71), 0)
    moe_gain = jnp.clip(1.0 + 0.18 * jax.random.normal(splits[8], (D,), jnp.float32), 0.1, 1.9)
    routes_keys = jax.random.split(jax.random.fold_in(splits[9], 1), REQS * NEW_TOK // ROWS_DEV)
    routes_turns = jax.random.permutation(jax.random.fold_in(splits[9], 3), REQS * NEW_TOK // ROWS_DEV)
    routes = jax.vmap(lambda own, number: routed_block(jax.random.fold_in(splits[9], 2), own, number, ROWS_DEV, EXPERTS, TOP, CAP, 1))(routes_keys, routes_turns).reshape((REQS, NEW_TOK, TOP))
    gate_weights = jnp.clip(0.1 + 0.59999999 * jax.random.uniform(splits[10], (REQS, NEW_TOK, TOP), jnp.float32) ** levels(splits[10], (REQS, NEW_TOK, TOP), ((0, 8),), -0.2, 0.2), 0.1, 0.7)
    w_gate_up = gaussian(splits[11], (EXPERTS, 2, D, FF), D ** -0.5, 0.109375, ((0, 8), (3, 4)))
    w_down = gaussian(splits[12], (EXPERTS, FF, D), FF ** -0.5, 0.109375, ((0, 8), (1, 4)))
    return {"tokens": tokens, "attn_gain": attn_gain, "w_qkv": w_qkv, "sink_logits": sink_logits, "w_out": w_out, "kv_cache": kv_cache, "page_table": page_table, "cache_lengths": cache_lengths, "moe_gain": moe_gain, "routes": routes, "gate_weights": gate_weights, "w_gate_up": w_gate_up, "w_down": w_down}


THETA_BASE = 150000.0
EPSILON = 1e-05
ALPHA_GLU = 1.702

def rms_scale(row_data, gain_vector):
    row_data = row_data.astype(jnp.float32)
    mean_square = lax.optimization_barrier(jnp.mean(row_data * row_data, axis=-1, keepdims=True))
    return row_data * lax.rsqrt(mean_square + EPSILON) * gain_vector

def rotate(vectors, positions):
    half_dim = vectors.shape[-1] // 2
    frequency = THETA_BASE ** (-(jnp.arange(half_dim, dtype=jnp.float32) * 2.0 / vectors.shape[-1]))
    angles = positions.astype(jnp.float32)[:, None] * frequency[None, :]
    view_shape = (vectors.shape[0],) + (1,) * (vectors.ndim - 2) + (half_dim,)
    cosine = jnp.cos(angles).reshape(view_shape)
    sine_part = jnp.sin(angles).reshape(view_shape)
    first_half = vectors[..., :half_dim]
    second_half = vectors[..., half_dim:]
    return jnp.concatenate([first_half * cosine - second_half * sine_part, second_half * cosine + first_half * sine_part], axis=-1)

def request_attention(tokens, kv_pages, cached_length, attn_gain, w_qkv, sink_logits, w_out):
    normed = rms_scale(tokens, attn_gain).astype(jnp.bfloat16)
    projected = jnp.dot(normed, w_qkv, preferred_element_type=jnp.float32).reshape(NEW_TOK, KVH, GROUP + 2, HD)
    positions = cached_length + jnp.arange(NEW_TOK, dtype=jnp.int32)
    queries = rotate(projected[:, :, :GROUP], positions).astype(jnp.bfloat16)
    new_keys = rotate(projected[:, :, GROUP], positions).astype(jnp.bfloat16)
    new_values = projected[:, :, GROUP + 1].astype(jnp.bfloat16)
    cached = kv_pages.reshape(CTX, KVH, 2, HD)
    all_keys = jnp.concatenate([cached[:, :, 0], new_keys], axis=0)
    all_values = jnp.concatenate([cached[:, :, 1], new_values], axis=0)
    key_position = jnp.arange(CTX + NEW_TOK, dtype=jnp.int32)
    query_position = jnp.arange(NEW_TOK, dtype=jnp.int32)
    visible = jnp.where(key_position[None, :] < CTX, key_position[None, :] < cached_length, key_position[None, :] - CTX <= query_position[:, None])
    score_scale = HD ** (-0.5)

    def head_attention(operands):
        query_head, key_head, value_head, sink_head = operands
        scores = jnp.einsum('qgd,kd->gqk', query_head.astype(jnp.float32), key_head.astype(jnp.float32)) * score_scale
        masked = jnp.where(visible[None], scores, -jnp.inf)
        peak = jnp.maximum(lax.optimization_barrier(jnp.max(masked, axis=-1)), sink_head[:, None])
        weights = jnp.where(visible[None], jnp.exp(scores - peak[..., None]), 0.0)
        denominator = lax.optimization_barrier(jnp.sum(weights, axis=-1)) + jnp.exp(sink_head[:, None] - peak)
        probs = weights.astype(jnp.bfloat16)
        numerator = jnp.einsum('gqk,kd->gqd', probs.astype(jnp.float32), value_head.astype(jnp.float32))
        return (numerator / denominator[..., None]).astype(jnp.bfloat16)
    attended = lax.map(head_attention, (queries.transpose(1, 0, 2, 3), all_keys.transpose(1, 0, 2), all_values.transpose(1, 0, 2), sink_logits.reshape(KVH, GROUP)))
    attended = attended.transpose(2, 0, 1, 3).reshape(NEW_TOK, QH * HD)
    return tokens.astype(jnp.float32) + jnp.dot(attended, w_out, preferred_element_type=jnp.float32)

def reference(tokens, attn_gain, w_qkv, sink_logits, w_out, kv_cache, page_table, cache_lengths, moe_gain, routes, gate_weights, w_gate_up, w_down):

    def per_request(request):
        kv_pages = kv_cache[request * PAGES_DEV + page_table[request]]
        return request_attention(tokens[request], kv_pages, cache_lengths[request], attn_gain, w_qkv, sink_logits, w_out)
    residual = lax.map(per_request, jnp.arange(REQS, dtype=jnp.int32)).reshape(REQS * NEW_TOK, D)
    moe_in = rms_scale(residual, moe_gain).astype(jnp.bfloat16)
    route_flat = routes.reshape(REQS * NEW_TOK, TOP)
    gate_flat = gate_weights.reshape(REQS * NEW_TOK, TOP)
    most_rows = N_REQ * N_KV * CAP

    def expert_pass(moe_sum, operands):
        expert, gate_up, down_proj = operands
        route_hit = route_flat == expert
        token_weight = lax.optimization_barrier(jnp.sum(jnp.where(route_hit, gate_flat, 0.0), axis=1))
        chosen = jnp.any(route_hit, axis=1)
        row_count = jnp.sum(chosen.astype(jnp.int32))
        row_index = jnp.nonzero(chosen, size=most_rows, fill_value=0)[0].astype(jnp.int32)
        in_range = jnp.arange(most_rows, dtype=jnp.int32) < row_count
        selected = moe_in[row_index]
        gate_part = jnp.dot(selected, gate_up[0], preferred_element_type=jnp.float32)
        up_part = jnp.dot(selected, gate_up[1], preferred_element_type=jnp.float32)
        activated = (gate_part * jax.nn.sigmoid(ALPHA_GLU * gate_part) * (up_part + 1.0)).astype(jnp.bfloat16)
        expert_out = jnp.dot(activated, down_proj, preferred_element_type=jnp.float32)
        scaled = jnp.where(in_range, token_weight[row_index], 0.0)[:, None] * expert_out
        return (moe_sum.at[row_index].add(scaled), None)
    mixed, unused = lax.scan(expert_pass, jnp.zeros((REQS * NEW_TOK, D), jnp.float32), (jnp.arange(EXPERTS, dtype=jnp.int32), w_gate_up, w_down))
    return (residual + mixed).astype(jnp.bfloat16).reshape(REQS, NEW_TOK, D)
```

```python
import functools

import jax
import jax.numpy as jnp
from jax import lax
from jax.experimental import pallas as pl
from jax.experimental.pallas import tpu as pltpu
from jax.sharding import PartitionSpec as P

HD = 64
TOP = 4
GROUP = 8


THETA_BASE = 150000.0
EPSILON = 1e-05
ALPHA_GLU = 1.702


def rms_scale(row_data, gain_vector):
    row_data = row_data.astype(jnp.float32)
    mean_square = jnp.mean(row_data * row_data, axis=-1, keepdims=True)
    return row_data * lax.rsqrt(mean_square + EPSILON) * gain_vector


def rotate(vectors, positions):
    half_dim = vectors.shape[-1] // 2
    frequency = THETA_BASE ** (-(jnp.arange(half_dim, dtype=jnp.float32) * 2.0 / vectors.shape[-1]))
    angles = positions.astype(jnp.float32)[:, None] * frequency[None, :]
    view_shape = (vectors.shape[0],) + (1,) * (vectors.ndim - 2) + (half_dim,)
    cosine = jnp.cos(angles).reshape(view_shape)
    sine_part = jnp.sin(angles).reshape(view_shape)
    first_half = vectors[..., :half_dim]
    second_half = vectors[..., half_dim:]
    return jnp.concatenate(
        [
            first_half * cosine - second_half * sine_part,
            second_half * cosine + first_half * sine_part,
        ],
        axis=-1,
    )


QUERY_CHUNK = 256


def attention_kernel(
    pages_ref, length_ref, query_ref, fresh_ref, sink_ref, *rest, new_count, page_size, page_step
):
    page_refs = rest[:page_step]
    out_ref, peak_ref, total_ref = rest[page_step:]
    heads, width, columns = query_ref.shape
    step = pl.program_id(0)
    length = length_ref[0]
    span = page_step * page_size
    chunk = min(QUERY_CHUNK, columns)

    def value_side(block):
        lane = lax.broadcasted_iota(jnp.int32, block.shape, 1)
        return jnp.where(lane < HD, jnp.ones_like(block), block)

    def weighted(block, weights):
        return lax.dot_general(
            block, weights, (((0,), (0,)), ((), ())), preferred_element_type=jnp.float32
        )

    @pl.when(step == 0)
    def _():
        key_at = lax.broadcasted_iota(jnp.int32, (new_count, columns), 0)
        query_at = lax.broadcasted_iota(jnp.int32, (new_count, columns), 1) % new_count
        causal = key_at <= query_at
        for head in range(heads):
            block = fresh_ref[:, head * width : (head + 1) * width]
            scores = jnp.dot(block, query_ref[head], preferred_element_type=jnp.float32)
            scores = jnp.where(causal, scores, -jnp.inf)
            sink = sink_ref[head : head + 1, :]
            peak = jnp.maximum(sink, jnp.max(scores, axis=0, keepdims=True))
            weights = jnp.exp(scores - peak).astype(jnp.bfloat16)
            row = lax.broadcasted_iota(jnp.int32, (width, columns), 0)
            start = jnp.where(row < HD, jnp.exp(sink - peak), 0.0)
            total_ref[head] = start + weighted(value_side(block), weights)
            peak_ref[head : head + 1, :] = peak

    def absorb(masked):
        for head in range(heads):
            block = jnp.concatenate(
                [page[0, :, head * width : (head + 1) * width] for page in page_refs], axis=0
            )
            value_block = value_side(block)
            for at in range(0, columns, chunk):
                part = slice(at, at + chunk)
                scores = jnp.dot(
                    block, query_ref[head, :, part], preferred_element_type=jnp.float32
                )
                if masked:
                    key_at = step * span + lax.broadcasted_iota(jnp.int32, scores.shape, 0)
                    scores = jnp.where(key_at < length, scores, -jnp.inf)
                old_peak = peak_ref[head : head + 1, part]
                peak = jnp.maximum(old_peak, jnp.max(scores, axis=0, keepdims=True))
                weights = jnp.exp(scores - peak).astype(jnp.bfloat16)
                total_ref[head, :, part] = total_ref[head, :, part] * jnp.exp(
                    old_peak - peak
                ) + weighted(value_block, weights)
                peak_ref[head : head + 1, part] = peak

    @pl.when((step + 1) * span <= length)
    def _():
        absorb(False)

    @pl.when(((step + 1) * span > length) & (step * span < length))
    def _():
        absorb(True)

    @pl.when(step == pl.num_programs(0) - 1)
    def _():
        for head in range(heads):
            total = total_ref[head]
            out_ref[head] = (total[HD:] / total[0:1]).astype(jnp.bfloat16)


def cache_attention(queries, new_block, sink_rows, kv_cache, page_row, cached_length):
    new_count, heads, group, _ = queries.shape
    page_size, cache_width = kv_cache.shape[1:]
    columns = group * new_count
    page_step = 8
    while page_row.shape[0] % page_step:
        page_step //= 2
    turned = (queries * jnp.bfloat16(HD**-0.5)).transpose(1, 3, 2, 0).reshape(heads, HD, columns)
    turned = jnp.concatenate([turned, jnp.zeros_like(turned)], axis=1)
    sink_columns = jnp.repeat(sink_rows, new_count, axis=1)
    fixed = lambda rank: (lambda step, pages, length: (0,) * rank)

    def page_spec(place):
        return pl.BlockSpec(
            (1, page_size, cache_width),
            lambda step, pages, length: (pages[step * page_step + place], 0, 0),
        )

    out = pl.pallas_call(
        functools.partial(
            attention_kernel, new_count=new_count, page_size=page_size, page_step=page_step
        ),
        grid_spec=pltpu.PrefetchScalarGridSpec(
            num_scalar_prefetch=2,
            grid=(page_row.shape[0] // page_step,),
            in_specs=[
                pl.BlockSpec((heads, 2 * HD, columns), fixed(3)),
                pl.BlockSpec((new_count, cache_width), fixed(2)),
                pl.BlockSpec((heads, columns), fixed(2)),
            ]
            + [page_spec(place) for place in range(page_step)],
            out_specs=pl.BlockSpec((heads, HD, columns), fixed(3)),
            scratch_shapes=[
                pltpu.VMEM((heads, columns), jnp.float32),
                pltpu.VMEM((heads, 2 * HD, columns), jnp.float32),
            ],
        ),
        out_shape=jax.ShapeDtypeStruct((heads, HD, columns), jnp.bfloat16),
        compiler_params=pltpu.CompilerParams(vmem_limit_bytes=40 * 1024 * 1024),
        name="cache_attention",
    )(page_row, cached_length, turned, new_block, sink_columns, *([kv_cache] * page_step))
    out = out.reshape(heads, HD, group, new_count).transpose(3, 0, 2, 1)
    return out.reshape(new_count, heads * group * HD)


def on_device(
    tokens,
    attn_gain,
    w_qkv,
    sink_logits,
    w_out,
    kv_cache,
    page_table,
    cache_lengths,
    moe_gain,
    routes,
    gate_weights,
    w_gate_up,
    w_down,
):
    kv_count = lax.axis_size("kv")
    req_count = lax.axis_size("req")
    place = lax.axis_index("kv")
    new_count = tokens.shape[1]
    rows_dev = new_count // kv_count
    heads_dev = w_qkv.shape[1] // ((GROUP + 2) * HD)
    own_tokens = tokens[0]
    experts_dev = w_gate_up.shape[0]
    experts_all = experts_dev * req_count
    hidden_dev = w_down.shape[1]

    chosen = routes[0][:, :, None] == jnp.arange(experts_all, dtype=jnp.int32)
    expert_gates = jnp.sum(jnp.where(chosen, gate_weights[0][:, :, None], 0.0), axis=1)
    all_gates = lax.all_gather(expert_gates, "req", axis=0, tiled=True)
    own_gates = lax.dynamic_slice_in_dim(
        all_gates, lax.axis_index("req") * experts_dev, experts_dev, 1
    )

    normed = rms_scale(own_tokens, attn_gain).astype(jnp.bfloat16)
    projected = jnp.dot(normed, w_qkv, preferred_element_type=jnp.float32).reshape(
        new_count, heads_dev, GROUP + 2, HD
    )
    positions = cache_lengths[0] + jnp.arange(new_count, dtype=jnp.int32)
    queries = rotate(projected[:, :, :GROUP], positions).astype(jnp.bfloat16)
    new_keys = rotate(projected[:, :, GROUP], positions).astype(jnp.bfloat16)
    new_values = projected[:, :, GROUP + 1].astype(jnp.bfloat16)
    new_block = jnp.concatenate([new_keys, new_values], axis=-1).reshape(new_count, -1)
    attended = cache_attention(
        queries,
        new_block,
        sink_logits.reshape(heads_dev, GROUP),
        kv_cache,
        page_table[0],
        cache_lengths,
    )

    partial_out = jnp.dot(attended, w_out, preferred_element_type=jnp.float32)
    summed_out = lax.psum_scatter(
        partial_out.astype(jnp.bfloat16), "kv", scatter_dimension=0, tiled=True
    ).astype(jnp.float32)
    own_rows = lax.dynamic_slice_in_dim(own_tokens, place * rows_dev, rows_dev, 0)
    residual = own_rows.astype(jnp.float32) + summed_out
    moe_rows = rms_scale(residual, moe_gain).astype(jnp.bfloat16)
    moe_in = lax.all_gather(moe_rows, ("req", "kv"), axis=0, tiled=True)
    hidden = []
    for expert in range(experts_dev):
        gate_part = jnp.dot(moe_in, w_gate_up[expert, 0], preferred_element_type=jnp.float32)
        up_part = jnp.dot(moe_in, w_gate_up[expert, 1], preferred_element_type=jnp.float32)
        activated = gate_part * jax.nn.sigmoid(ALPHA_GLU * gate_part) * (up_part + 1.0)
        hidden.append((activated * own_gates[:, expert : expert + 1]).astype(jnp.bfloat16))
    mixed_part = jnp.dot(
        jnp.concatenate(hidden, axis=1),
        w_down.reshape(experts_dev * hidden_dev, -1),
        preferred_element_type=jnp.float32,
    ).astype(jnp.bfloat16)
    mixture = lax.psum_scatter(
        mixed_part, ("req", "kv"), scatter_dimension=0, tiled=True
    ).astype(jnp.float32)
    return (residual + mixture).astype(jnp.bfloat16)[None]


def solution(mesh):
    in_specs = (
        P("req", None, None),
        P(),
        P(None, "kv"),
        P("kv"),
        P("kv", None),
        P("req", None, "kv"),
        P("req", None),
        P("req"),
        P(),
        P("req", None, None),
        P("req", None, None),
        P("req", None, None, "kv"),
        P("req", "kv", None),
    )
    out_specs = P("req", "kv", None)
    return jax.shard_map(
        on_device, mesh=mesh, in_specs=in_specs, out_specs=out_specs, check_vma=False
    )
```

```python
import functools

import jax
import jax.numpy as jnp
from jax import lax
from jax.experimental import pallas as pl
from jax.experimental.pallas import tpu as pltpu
from jax.sharding import PartitionSpec as P

HD = 64
TOP = 4
GROUP = 8


THETA_BASE = 150000.0
EPSILON = 1e-05
ALPHA_GLU = 1.702


def rms_scale(row_data, gain_vector):
    row_data = row_data.astype(jnp.float32)
    mean_square = jnp.mean(row_data * row_data, axis=-1, keepdims=True)
    return row_data * lax.rsqrt(mean_square + EPSILON) * gain_vector


def rotate(vectors, positions):
    half_dim = vectors.shape[-1] // 2
    frequency = THETA_BASE ** (-(jnp.arange(half_dim, dtype=jnp.float32) * 2.0 / vectors.shape[-1]))
    angles = positions.astype(jnp.float32)[:, None] * frequency[None, :]
    view_shape = (vectors.shape[0],) + (1,) * (vectors.ndim - 2) + (half_dim,)
    cosine = jnp.cos(angles).reshape(view_shape)
    sine_part = jnp.sin(angles).reshape(view_shape)
    first_half = vectors[..., :half_dim]
    second_half = vectors[..., half_dim:]
    return jnp.concatenate(
        [
            first_half * cosine - second_half * sine_part,
            second_half * cosine + first_half * sine_part,
        ],
        axis=-1,
    )


QUERY_CHUNK = 256


def attention_kernel(
    pages_ref, length_ref, query_ref, fresh_ref, sink_ref, *rest, new_count, page_size, page_step
):
    page_refs = rest[:page_step]
    out_ref, peak_ref, total_ref = rest[page_step:]
    heads, width, columns = query_ref.shape
    step = pl.program_id(0)
    length = length_ref[0]
    span = page_step * page_size
    chunk = min(QUERY_CHUNK, columns)

    def value_side(block):
        lane = lax.broadcasted_iota(jnp.int32, block.shape, 1)
        return jnp.where(lane < HD, jnp.ones_like(block), block)

    def weighted(block, weights):
        return lax.dot_general(
            block, weights, (((0,), (0,)), ((), ())), preferred_element_type=jnp.float32
        )

    @pl.when(step == 0)
    def _():
        key_at = lax.broadcasted_iota(jnp.int32, (new_count, columns), 0)
        query_at = lax.broadcasted_iota(jnp.int32, (new_count, columns), 1) % new_count
        causal = key_at <= query_at
        for head in range(heads):
            block = fresh_ref[:, head * width : (head + 1) * width]
            scores = jnp.dot(block, query_ref[head], preferred_element_type=jnp.float32)
            scores = jnp.where(causal, scores, -jnp.inf)
            sink = sink_ref[head : head + 1, :]
            peak = jnp.maximum(sink, jnp.max(scores, axis=0, keepdims=True))
            weights = jnp.exp(scores - peak).astype(jnp.bfloat16)
            row = lax.broadcasted_iota(jnp.int32, (width, columns), 0)
            start = jnp.where(row < HD, jnp.exp(sink - peak), 0.0)
            total_ref[head] = start + weighted(value_side(block), weights)
            peak_ref[head : head + 1, :] = peak

    def absorb(masked):
        for head in range(heads):
            block = jnp.concatenate(
                [page[0, :, head * width : (head + 1) * width] for page in page_refs], axis=0
            )
            value_block = value_side(block)
            for at in range(0, columns, chunk):
                part = slice(at, at + chunk)
                scores = jnp.dot(
                    block, query_ref[head, :, part], preferred_element_type=jnp.float32
                )
                if masked:
                    key_at = step * span + lax.broadcasted_iota(jnp.int32, scores.shape, 0)
                    scores = jnp.where(key_at < length, scores, -jnp.inf)
                old_peak = peak_ref[head : head + 1, part]
                peak = jnp.maximum(old_peak, jnp.max(scores, axis=0, keepdims=True))
                weights = jnp.exp(scores - peak).astype(jnp.bfloat16)
                total_ref[head, :, part] = total_ref[head, :, part] * jnp.exp(
                    old_peak - peak
                ) + weighted(value_block, weights)
                peak_ref[head : head + 1, part] = peak

    @pl.when((step + 1) * span <= length)
    def _():
        absorb(False)

    @pl.when(((step + 1) * span > length) & (step * span < length))
    def _():
        absorb(True)

    @pl.when(step == pl.num_programs(0) - 1)
    def _():
        for head in range(heads):
            total = total_ref[head]
            out_ref[head] = (total[HD:] / total[0:1]).astype(jnp.bfloat16)


def cache_attention(queries, new_block, sink_rows, kv_cache, page_row, cached_length):
    new_count, heads, group, _ = queries.shape
    page_size, cache_width = kv_cache.shape[1:]
    columns = group * new_count
    page_step = 8
    while page_row.shape[0] % page_step:
        page_step //= 2
    turned = (queries * jnp.bfloat16(HD**-0.5)).transpose(1, 3, 2, 0).reshape(heads, HD, columns)
    turned = jnp.concatenate([turned, jnp.zeros_like(turned)], axis=1)
    sink_columns = jnp.repeat(sink_rows, new_count, axis=1)
    fixed = lambda rank: (lambda step, pages, length: (0,) * rank)

    def page_spec(place):
        return pl.BlockSpec(
            (1, page_size, cache_width),
            lambda step, pages, length: (pages[step * page_step + place], 0, 0),
        )

    out = pl.pallas_call(
        functools.partial(
            attention_kernel, new_count=new_count, page_size=page_size, page_step=page_step
        ),
        grid_spec=pltpu.PrefetchScalarGridSpec(
            num_scalar_prefetch=2,
            grid=(page_row.shape[0] // page_step,),
            in_specs=[
                pl.BlockSpec((heads, 2 * HD, columns), fixed(3)),
                pl.BlockSpec((new_count, cache_width), fixed(2)),
                pl.BlockSpec((heads, columns), fixed(2)),
            ]
            + [page_spec(place) for place in range(page_step)],
            out_specs=pl.BlockSpec((heads, HD, columns), fixed(3)),
            scratch_shapes=[
                pltpu.VMEM((heads, columns), jnp.float32),
                pltpu.VMEM((heads, 2 * HD, columns), jnp.float32),
            ],
        ),
        out_shape=jax.ShapeDtypeStruct((heads, HD, columns), jnp.bfloat16),
        compiler_params=pltpu.CompilerParams(vmem_limit_bytes=40 * 1024 * 1024),
        name="cache_attention",
    )(page_row, cached_length, turned, new_block, sink_columns, *([kv_cache] * page_step))
    out = out.reshape(heads, HD, group, new_count).transpose(3, 0, 2, 1)
    return out.reshape(new_count, heads * group * HD)


def on_device(
    tokens,
    attn_gain,
    w_qkv,
    sink_logits,
    w_out,
    kv_cache,
    page_table,
    cache_lengths,
    moe_gain,
    routes,
    gate_weights,
    w_gate_up,
    w_down,
):
    kv_count = lax.axis_size("kv")
    req_count = lax.axis_size("req")
    place = lax.axis_index("kv")
    new_count = tokens.shape[1]
    rows_dev = new_count // kv_count
    heads_dev = w_qkv.shape[1] // ((GROUP + 2) * HD)
    own_tokens = tokens[0]
    experts_dev = w_gate_up.shape[0]
    experts_all = experts_dev * req_count
    hidden_dev = w_down.shape[1]

    chosen = routes[0][:, :, None] == jnp.arange(experts_all, dtype=jnp.int32)
    expert_gates = jnp.sum(jnp.where(chosen, gate_weights[0][:, :, None], 0.0), axis=1)
    all_gates = lax.all_gather(expert_gates, "req", axis=0, tiled=True)
    own_gates = lax.dynamic_slice_in_dim(
        all_gates, lax.axis_index("req") * experts_dev, experts_dev, 1
    )

    normed = rms_scale(own_tokens, attn_gain).astype(jnp.bfloat16)
    projected = jnp.dot(normed, w_qkv, preferred_element_type=jnp.float32).reshape(
        new_count, heads_dev, GROUP + 2, HD
    )
    positions = cache_lengths[0] + jnp.arange(new_count, dtype=jnp.int32)
    queries = rotate(projected[:, :, :GROUP], positions).astype(jnp.bfloat16)
    new_keys = rotate(projected[:, :, GROUP], positions).astype(jnp.bfloat16)
    new_values = projected[:, :, GROUP + 1].astype(jnp.bfloat16)
    new_block = jnp.concatenate([new_keys, new_values], axis=-1).reshape(new_count, -1)
    attended = cache_attention(
        queries,
        new_block,
        sink_logits.reshape(heads_dev, GROUP),
        kv_cache,
        page_table[0],
        cache_lengths,
    )

    partial_out = jnp.dot(attended, w_out, preferred_element_type=jnp.float32)
    summed_out = lax.psum_scatter(
        partial_out.astype(jnp.bfloat16), "kv", scatter_dimension=0, tiled=True
    ).astype(jnp.float32)
    own_rows = lax.dynamic_slice_in_dim(own_tokens, place * rows_dev, rows_dev, 0)
    residual = own_rows.astype(jnp.float32) + summed_out
    moe_rows = rms_scale(residual, moe_gain).astype(jnp.bfloat16)
    moe_in = lax.all_gather(moe_rows, ("req", "kv"), axis=0, tiled=True)
    hidden = []
    for expert in range(experts_dev):
        gate_part = jnp.dot(moe_in, w_gate_up[expert, 0], preferred_element_type=jnp.float32)
        up_part = jnp.dot(moe_in, w_gate_up[expert, 1], preferred_element_type=jnp.float32)
        activated = gate_part * jax.nn.sigmoid(ALPHA_GLU * gate_part) * (up_part + 1.0)
        hidden.append((activated * own_gates[:, expert : expert + 1]).astype(jnp.bfloat16))
    mixed_part = jnp.dot(
        jnp.concatenate(hidden, axis=1),
        w_down.reshape(experts_dev * hidden_dev, -1),
        preferred_element_type=jnp.float32,
    ).astype(jnp.bfloat16)
    parts = mixed_part.reshape(req_count, kv_count, rows_dev, -1).transpose(1, 0, 2, 3)
    parts = lax.all_to_all(parts, "kv", split_axis=0, concat_axis=0, tiled=True)
    hidden_sum = jnp.sum(parts.astype(jnp.float32), axis=0).astype(jnp.bfloat16)
    expert_parts = lax.all_to_all(hidden_sum, "req", split_axis=0, concat_axis=0, tiled=True)
    mixture = jnp.sum(expert_parts.astype(jnp.float32), axis=0)
    return (residual + mixture).astype(jnp.bfloat16)[None]


def solution(mesh):
    in_specs = (
        P("req", None, None),
        P(),
        P(None, "kv"),
        P("kv"),
        P("kv", None),
        P("req", None, "kv"),
        P("req", None),
        P("req"),
        P(),
        P("req", None, None),
        P("req", None, None),
        P("req", None, None, "kv"),
        P("req", "kv", None),
    )
    out_specs = P("req", "kv", None)
    return jax.shard_map(
        on_device, mesh=mesh, in_specs=in_specs, out_specs=out_specs, check_vma=False
    )
```
